32 devices in a mesh: grp: 2 (over y), seq: 16 (over z, x, core).
Axes of the slice: x: 2, y: 2, z: 4, core: 2. Of those that a mesh axis runs over, the one named last changes fastest.
Arguments:
- query: bfloat16 [4096, 2560], P(('grp', 'seq')), parts along dimension 0, may hold values from -6 to 6
- key: bfloat16 [4096, 2560], P(('grp', 'seq')), parts along dimension 0, may hold values from -6 to 6
- value: bfloat16 [4096, 2560], P(('grp', 'seq')), parts along dimension 0, may hold values from -6 to 6
- grad_out: bfloat16 [4096, 2560], P(('grp', 'seq')), parts along dimension 0, may hold values from -6 to 6
- tile_mask: int32 [16, 7, 1, 1], P('seq'), may hold values from 0 to 1, as said below
Outputs:
- attended: bfloat16 [4096, 2560], P(('grp', 'seq')), parts along dimension 0
- grad_query: bfloat16 [4096, 2560], P(('grp', 'seq')), parts along dimension 0
- grad_key: bfloat16 [4096, 2560], P(('grp', 'seq')), parts along dimension 0
- grad_value: bfloat16 [4096, 2560], P(('grp', 'seq')), parts along dimension 0
The draws below stay inside these ranges and needn't reach their ends.
There are 2 independent parts, one for each index of `grp`. The reference program is written for one: setup_inputs(seed, part) draws one part's arguments, and reference() takes and returns one part's arrays. A program takes and returns all parts, laid end to end along the dimension named above; an argument that names none is the same for every part. Nothing has to cross between parts.
Inputs may be any that keep to these rules, and one draw needn't show every extreme that they name: tile_mask[i, d, a, b] allows query tile a of shard i to attend to key tile b of shard i + o_d, with o_0 = 0, o_(2k+1) = 2**k, o_(2k+2) = -2**k; offset 0 is all ones; entries toward shards outside the sequence are 0.
All inputs are finite; a program needn't handle non-finite values.
Results may differ from the reference program's by a relative error of at most 0.019.
Values may be sent and summed in bfloat16 or wider, within the bound.
A program may use at most 128 MiB of HBM per device.

```python
import jax
import jax.numpy as jnp
from jax import lax

HEADS = 20
HEAD = 128
TILE = 128
LEVELS = 3
ROWS_DEV = 128
HD = 2560
DISTS = 7
TB = 1
TOKENS = 2048
N_SEQ = 16


def base_rows(key):
    return jnp.clip(jax.random.normal(key, (TOKENS, HEADS * HEAD), jnp.float32), -6.0, 6.0)


def draw_query(key, part):
    values = base_rows(jax.random.fold_in(key, 21))
    return values.astype(jnp.bfloat16)


def draw_key(key, part):
    values = base_rows(jax.random.fold_in(key, 22))
    return values.astype(jnp.bfloat16)


def draw_tile_mask(key, part):
    offsets = jnp.array([0] + [direction * 2 ** level_index for level_index in range(LEVELS) for direction in (1, -1)], jnp.int32)
    divisor = jnp.array([1] + [level_index + 2 for level_index in range(LEVELS) for direction in (1, -1)], jnp.int32)
    ticket = jax.random.randint(jax.random.fold_in(key, 11), (N_SEQ, DISTS, TB, TB), 0, 60)
    keeping = ticket % divisor[None, :, None, None] == 0
    partner = jnp.arange(N_SEQ, dtype=jnp.int32)[:, None] + offsets[None, :]
    inside = (partner >= 0) & (partner < N_SEQ)
    return (keeping & inside[:, :, None, None]).astype(jnp.int32)


def block_levels(key, dims, pieces, least, largest):
    level, own = 1.0, jax.random.fold_in(key, 6)
    for position, parts in pieces:
        heights = jnp.exp(jax.random.uniform(jax.random.fold_in(own, position), (parts,), jnp.float32, least / len(pieces), largest / len(pieces)))
        level = level * jnp.repeat(heights, dims[position] // parts).reshape([-1 if axis == position else 1 for axis in range(len(dims))])
    return level


def centred(own_key, extent, deviation, bound, shards=(), kind=jnp.bfloat16):
    factor_of = block_levels(own_key, extent, shards, -0.22, 0.18) if shards else 1.0
    values = jax.random.normal(own_key, extent, jnp.float32) * deviation * factor_of
    return jnp.minimum(jnp.maximum(values, -bound), bound).astype(kind)


def setup_inputs(seed: int = 0, part: int = 0) -> dict:
    key_list = jax.random.split(jax.random.key(seed), 6)
    part_splits = jax.random.split(jax.random.fold_in(key_list[5], part), 6)
    query = draw_query(jax.random.fold_in(jax.random.fold_in(key_list[5], part), 71), part)
    key = draw_key(jax.random.fold_in(jax.random.fold_in(key_list[5], part), 71), part)
    value = centred(part_splits[2], (TOKENS, HD), 1.0, 6.0, ((0, 16),))
    grad_out = centred(part_splits[3], (TOKENS, HD), 1.0, 6.0, ((0, 16),))
    tile_mask = draw_tile_mask(jax.random.fold_in(key_list[5], 71), part)
    return dict(query=query, key=key, value=value, grad_out=grad_out, tile_mask=tile_mask)


NEG = -1.0e30


def offset_list(level_total):
    return [0] + [direction * 2 ** level_index for level_index in range(level_total) for direction in (1, -1)]


def shift_rows(array, offset):
    shard_total = array.shape[0]
    if offset == 0:
        return array
    padding = jnp.zeros((abs(offset),) + array.shape[1:], array.dtype)
    if offset > 0:
        return jnp.concatenate([array[offset:], padding], 0)
    return jnp.concatenate([padding, array[:shard_total + offset]], 0)


def narrow(array):
    return lax.optimization_barrier(array.astype(jnp.bfloat16)).astype(jnp.float32)


def expand(tile_mask, dist_index):
    flags = tile_mask[:, dist_index]
    full_mask = jnp.broadcast_to(flags[:, :, None, :, None], (N_SEQ, TB, TILE, TB, TILE)).reshape(N_SEQ, ROWS_DEV, ROWS_DEV)
    return (full_mask > 0)[:, None]


def reference(query, key, value, grad_out, tile_mask):
    shape4 = (N_SEQ, ROWS_DEV, HEADS, HEAD)
    query_f = query.reshape(shape4).astype(jnp.float32)
    key_f = key.reshape(shape4).astype(jnp.float32)
    value_f = value.reshape(shape4).astype(jnp.float32)
    grad_f = grad_out.reshape(shape4).astype(jnp.float32)
    score_scale = HEAD ** -0.5
    offsets = offset_list(LEVELS)

    def masked_scores(dist_index, offset):
        remote = shift_rows(key_f, offset)
        scores = jnp.einsum("nqhd,nkhd->nhqk", query_f, remote) * score_scale
        allowed = expand(tile_mask, dist_index)
        return allowed, jnp.where(allowed, scores, NEG)

    top = jnp.full((N_SEQ, HEADS, ROWS_DEV), NEG, jnp.float32)
    total = jnp.zeros((N_SEQ, HEADS, ROWS_DEV), jnp.float32)
    for dist_index, offset in enumerate(offsets):
        allowed, scores = masked_scores(dist_index, offset)
        newtop = jnp.maximum(top, jnp.max(scores, -1))
        total = total * jnp.exp(top - newtop) + jnp.sum(jnp.exp(scores - newtop[..., None]), -1)
        top = newtop
    log_total = top + jnp.log(total)

    out_acc = jnp.zeros(shape4, jnp.float32)
    for dist_index, offset in enumerate(offsets):
        allowed, scores = masked_scores(dist_index, offset)
        probs = narrow(jnp.where(allowed, jnp.exp(scores - log_total[..., None]), 0.0))
        out_acc = out_acc + jnp.einsum("nhqk,nkhd->nqhd", probs, shift_rows(value_f, offset))
    attended = out_acc.astype(jnp.bfloat16)

    delta = jnp.sum(grad_f * attended.astype(jnp.float32), -1)
    delta = jnp.transpose(delta, (0, 2, 1))
    query_acc = jnp.zeros(shape4, jnp.float32)
    key_acc = jnp.zeros(shape4, jnp.float32)
    value_acc = jnp.zeros(shape4, jnp.float32)
    for dist_index, offset in enumerate(offsets):
        allowed, scores = masked_scores(dist_index, offset)
        exact = jnp.where(allowed, jnp.exp(scores - log_total[..., None]), 0.0)
        probs = narrow(exact)
        remote_keys = shift_rows(key_f, offset)
        remote_values = shift_rows(value_f, offset)
        dprobs = jnp.einsum("nqhd,nkhd->nhqk", grad_f, remote_values)
        dscores = narrow(exact * (dprobs - delta[..., None]))
        query_acc = query_acc + jnp.einsum("nhqk,nkhd->nqhd", dscores, remote_keys)
        key_part = jnp.einsum("nhqk,nqhd->nkhd", dscores, query_f) * score_scale
        value_part = jnp.einsum("nhqk,nqhd->nkhd", probs, grad_f)
        if offset != 0:
            key_part = narrow(key_part)
            value_part = narrow(value_part)
        key_acc = key_acc + shift_rows(key_part, -offset)
        value_acc = value_acc + shift_rows(value_part, -offset)
    flat = (N_SEQ * ROWS_DEV, HEADS * HEAD)
    grad_query = (query_acc * score_scale).reshape(flat).astype(jnp.bfloat16)
    grad_key = key_acc.reshape(flat).astype(jnp.bfloat16)
    grad_value = value_acc.reshape(flat).astype(jnp.bfloat16)
    return (attended.reshape(flat), grad_query, grad_key, grad_value)
```

```python
import functools

import jax
import jax.numpy as jnp
from jax import lax
from jax.experimental import pallas as pl
from jax.experimental.pallas import tpu as pltpu
from jax.sharding import PartitionSpec as P

HEAD = 128
HEADS_CHUNK = 4
BIG = 1e30
AHEAD = 2

OWN, SIB, CROSS, NEAR, DIAG, ZF, ZB = range(7)
C_SIB, C_CROSS, C_NEAR, C_DIAG_A, C_DIAG_B, C_ZF, C_ZB = range(7)
NT = (((1,), (1,)), ((), ()))


def kernel(seq, mask_ref, q_ref, k_ref, v_ref, g_ref, att_ref, gq_ref, gk_ref, gv_ref,
           rb, bias, stat_s, stat_r, load_sem, send_sem, recv_sem, stat_send, stat_recv):
    rows = q_ref.shape[0]
    width = HEADS_CHUNK * HEAD
    chunks = q_ref.shape[1] // width
    steps = 2 * chunks
    scale = HEAD ** (-0.5)

    me = lax.axis_index("seq")
    core = lax.rem(me, 2)
    parity = lax.rem(lax.div(me, 2), 2)
    s = 1 - 2 * parity
    sib = me + 1 - 2 * core
    cross = me - 1 + 2 * core
    near, diag, zf, zb = me + 2 * s, me - 2 * s, me + 4 * s, me - 4 * s
    cross_ok = jnp.logical_and(cross >= 0, cross < seq)
    zf_ok = jnp.logical_and(zf >= 0, zf < seq)
    zb_ok = jnp.logical_and(zb >= 0, zb < seq)
    cross_send_ok = jnp.logical_or(core == parity, zb_ok)
    cross_src = jnp.where(core == parity, NEAR, DIAG)
    always = me >= 0
    target = {SIB: sib, CROSS: cross, NEAR: near, DIAG: diag, ZF: zf, ZB: zb}
    exists = {SIB: always, CROSS: cross_ok, NEAR: always, DIAG: zb_ok, ZF: zf_ok, ZB: zb_ok}
    reverse = {SIB: SIB, CROSS: CROSS, NEAR: NEAR, DIAG: DIAG, ZF: ZB, ZB: ZF}
    dist = {
        OWN: 0, SIB: 1 + core, CROSS: 2 - core, NEAR: 3 + parity, DIAG: 4 - parity,
        ZF: 5 + parity, ZB: 6 - parity,
    }

    def loads():
        return [
            pltpu.make_async_copy(ref, rb.at[OWN, j], load_sem.at[j])
            for j, ref in enumerate((k_ref, v_ref, q_ref, g_ref))
        ]

    for copy in loads():
        copy.start()

    barrier = pltpu.get_barrier_semaphore()
    for slot in (SIB, CROSS, NEAR, DIAG, ZF, ZB):
        @pl.when(exists[slot])
        def _(slot=slot):
            pl.semaphore_signal(barrier, inc=1, device_id={"seq": target[slot]})

    for slot in range(7):
        amount = (1.0 - mask_ref[dist[slot]].astype(jnp.float32)) * BIG
        bias[slot] = jnp.zeros((8, 128), jnp.float32) + amount

    for slot in (CROSS, DIAG, ZF, ZB):
        @pl.when(jnp.logical_not(exists[slot]))
        def _(slot=slot):
            rb[slot] = jnp.zeros(rb.shape[1:], rb.dtype)
            stat_r[slot] = jnp.full(stat_r.shape[1:], BIG, jnp.float32)

    peers = sum(jnp.where(exists[slot], 1, 0) for slot in (SIB, CROSS, NEAR, DIAG, ZF, ZB))
    pl.semaphore_wait(barrier, peers)

    def pair(slot, t):
        cols = pl.ds(pl.multiple_of(lax.rem(t, chunks) * width, width), width)
        return rb.at[slot, pl.ds(2 * lax.div(t, chunks), 2), :, cols]

    def half(slot, which, t):
        cols = pl.ds(pl.multiple_of(lax.rem(t, chunks) * width, width), width)
        return rb.at[slot, 2 * lax.div(t, chunks) + which, :, cols]

    def copy_of(kind, t):
        if kind == C_SIB:
            src, dst, device = pair(OWN, t), pair(SIB, t), sib
        elif kind == C_NEAR:
            src, dst, device = pair(OWN, t), pair(NEAR, t), near
        elif kind == C_ZB:
            src, dst, device = pair(OWN, t), pair(ZB, t), zf
        elif kind == C_ZF:
            src, dst, device = pair(OWN, t), pair(ZF, t), zb
        elif kind == C_DIAG_A:
            src, dst, device = half(NEAR, 0, t), half(DIAG, 0, t), zf
        elif kind == C_DIAG_B:
            src, dst, device = half(ZF, 1, t), half(DIAG, 1, t), near
        else:
            src, dst, device = pair(cross_src, t), pair(CROSS, t), sib
        return pltpu.make_async_remote_copy(
            src_ref=src, dst_ref=dst, send_sem=send_sem.at[kind, t], recv_sem=recv_sem.at[kind, t],
            device_id={"seq": device}, device_id_type=pl.DeviceIdType.MESH,
        )

    sends = {
        C_SIB: always, C_CROSS: cross_send_ok, C_NEAR: always, C_DIAG_A: zf_ok, C_DIAG_B: zf_ok,
        C_ZF: zb_ok, C_ZB: zf_ok,
    }
    receives = {
        C_SIB: always, C_CROSS: cross_ok, C_NEAR: always, C_DIAG_A: zb_ok, C_DIAG_B: zb_ok,
        C_ZF: zf_ok, C_ZB: zb_ok,
    }

    def start(kind, t):
        @pl.when(sends[kind])
        def _():
            copy_of(kind, t).start()

    def arrived(kind, t):
        @pl.when(receives[kind])
        def _():
            copy_of(kind, t).wait_recv()

    def direct(t):
        for kind in (C_ZB, C_ZF, C_NEAR, C_SIB):
            start(kind, t)

    def stat_copy(slot, chunk):
        return pltpu.make_async_remote_copy(
            src_ref=stat_s.at[slot, chunk], dst_ref=stat_r.at[reverse[slot], chunk],
            send_sem=stat_send.at[slot, chunk], recv_sem=stat_recv.at[reverse[slot], chunk],
            device_id={"seq": target[slot]}, device_id_type=pl.DeviceIdType.MESH,
        )

    def stat_arrival(slot, chunk):
        return pltpu.make_async_remote_copy(
            src_ref=stat_s.at[slot, chunk], dst_ref=stat_r.at[slot, chunk],
            send_sem=stat_send.at[slot, chunk], recv_sem=stat_recv.at[slot, chunk],
            device_id={"seq": target[slot]}, device_id_type=pl.DeviceIdType.MESH,
        )

    def stacked(tensor, cols):
        return rb[:, tensor, :, cols].reshape(7 * rows, HEAD)

    def query_side(chunk):
        lane = lax.broadcasted_iota(jnp.int32, (rows, 128), 1)
        stats = jnp.zeros((rows, 128), jnp.float32)
        shift = jnp.concatenate([bias[slot][:1, :] for slot in range(7)], axis=1)
        for index in range(HEADS_CHUNK):
            cols = pl.ds(pl.multiple_of(chunk * width + index * HEAD, HEAD), HEAD)
            keys, values = stacked(0, cols), stacked(1, cols)
            queries, grads = rb[OWN, 2, :, cols], rb[OWN, 3, :, cols]
            scores = lax.dot_general(queries, keys, NT, preferred_element_type=jnp.float32)
            scores = scores * scale - shift
            top = jnp.max(scores, axis=1, keepdims=True)
            weights = jnp.exp(scores - top)
            total = jnp.sum(weights, axis=1, keepdims=True)
            exact = weights * (1.0 / total)
            out = jnp.dot(exact.astype(jnp.bfloat16), values, preferred_element_type=jnp.float32)
            out = out.astype(jnp.bfloat16)
            att_ref[:, cols] = out
            delta = jnp.sum(grads.astype(jnp.float32) * out.astype(jnp.float32), axis=1, keepdims=True)
            dprobs = lax.dot_general(grads, values, NT, preferred_element_type=jnp.float32)
            dscores = (exact * (dprobs - delta)).astype(jnp.bfloat16)
            grad = jnp.dot(dscores, keys, preferred_element_type=jnp.float32) * scale
            gq_ref[:, cols] = grad.astype(jnp.bfloat16)
            stats = jnp.where(lane == index, top + jnp.log(total), stats)
            stats = jnp.where(lane == index + 8, delta, stats)
        turned = jnp.transpose(stats)
        lse, delta = turned[:8], turned[8:16]
        stat_r[OWN, chunk] = jnp.concatenate([lse, delta], axis=0)
        for slot in (SIB, CROSS, NEAR, DIAG, ZF, ZB):
            stat_s[slot, chunk] = jnp.concatenate([lse + bias[slot], delta], axis=0)
        for slot in (SIB, CROSS, NEAR, DIAG, ZF, ZB):
            @pl.when(exists[slot])
            def _(slot=slot):
                stat_copy(slot, chunk).start()

    def key_side(chunk):
        for slot in (SIB, CROSS, NEAR, DIAG, ZF, ZB):
            @pl.when(exists[slot])
            def _(slot=slot):
                stat_arrival(slot, chunk).wait_recv()
        stats = jnp.concatenate([stat_r[slot, chunk] for slot in range(7)], axis=1)
        for index in range(HEADS_CHUNK):
            cols = pl.ds(pl.multiple_of(chunk * width + index * HEAD, HEAD), HEAD)
            queries, grads = stacked(2, cols), stacked(3, cols)
            keys, values = rb[OWN, 0, :, cols], rb[OWN, 1, :, cols]
            lse, delta = stats[index:index + 1], stats[index + 8:index + 9]
            scores = lax.dot_general(keys, queries, NT, preferred_element_type=jnp.float32)
            exact = jnp.exp(scores * scale - lse)
            value_grad = jnp.dot(exact.astype(jnp.bfloat16), grads, preferred_element_type=jnp.float32)
            gv_ref[:, cols] = value_grad.astype(jnp.bfloat16)
            dprobs = lax.dot_general(values, grads, NT, preferred_element_type=jnp.float32)
            dscores = (exact * (dprobs - delta)).astype(jnp.bfloat16)
            key_grad = jnp.dot(dscores, queries, preferred_element_type=jnp.float32) * scale
            gk_ref[:, cols] = key_grad.astype(jnp.bfloat16)

    for copy in loads():
        copy.wait()
    for t in range(AHEAD):
        direct(jnp.int32(t))

    def step(t, carry):
        @pl.when(t + AHEAD < steps)
        def _():
            direct(t + AHEAD)

        @pl.when(t < steps)
        def _():
            arrived(C_NEAR, t)
            start(C_DIAG_A, t)
            arrived(C_ZF, t)
            start(C_DIAG_B, t)

        @pl.when(jnp.logical_and(t >= 1, t <= steps))
        def _():
            arrived(C_DIAG_A, t - 1)
            arrived(C_DIAG_B, t - 1)
            start(C_CROSS, t - 1)

        @pl.when(t >= 2)
        def _():
            arrived(C_SIB, t - 2)
            arrived(C_ZB, t - 2)
            arrived(C_CROSS, t - 2)

        @pl.when(jnp.logical_and(t >= 2, t - 2 < chunks))
        def _():
            query_side(t - 2)

        @pl.when(t - 2 >= chunks)
        def _():
            key_side(t - 2 - chunks)

        return carry

    lax.fori_loop(0, steps + 2, step, 0)

    def drain(t, carry):
        for kind in range(7):
            @pl.when(sends[kind])
            def _(kind=kind):
                copy_of(kind, t).wait_send()
        return carry

    lax.fori_loop(0, steps, drain, 0)

    def drain_stats(chunk, carry):
        for slot in (SIB, CROSS, NEAR, DIAG, ZF, ZB):
            @pl.when(exists[slot])
            def _(slot=slot):
                stat_copy(slot, chunk).wait_send()
        return carry

    lax.fori_loop(0, chunks, drain_stats, 0)


def local(seq, query, key, value, grad_out, tile_mask):
    rows, features = query.shape
    chunks = features // (HEADS_CHUNK * HEAD)
    shape = jax.ShapeDtypeStruct((rows, features), jnp.bfloat16)
    vmem = pl.BlockSpec(memory_space=pltpu.VMEM)
    anywhere = pl.BlockSpec(memory_space=pl.ANY)
    pairs = rows * rows * features * 7
    return pl.pallas_call(
        functools.partial(kernel, seq),
        name="radial",
        out_shape=(shape,) * 4,
        in_specs=[pl.BlockSpec(memory_space=pltpu.SMEM)] + [anywhere] * 4,
        out_specs=(vmem,) * 4,
        scratch_shapes=[
            pltpu.VMEM((7, 4, rows, features), jnp.bfloat16),
            pltpu.VMEM((7, 8, 128), jnp.float32),
            pltpu.VMEM((7, chunks, 16, 128), jnp.float32),
            pltpu.VMEM((7, chunks, 16, 128), jnp.float32),
            pltpu.SemaphoreType.DMA((4,)),
            pltpu.SemaphoreType.DMA((7, 2 * chunks)),
            pltpu.SemaphoreType.DMA((7, 2 * chunks)),
            pltpu.SemaphoreType.DMA((7, chunks)),
            pltpu.SemaphoreType.DMA((7, chunks)),
        ],
        compiler_params=pltpu.CompilerParams(
            collective_id=0, has_side_effects=True, vmem_limit_bytes=48 << 20
        ),
        cost_estimate=pl.CostEstimate(
            flops=16 * pairs, transcendentals=2 * pairs // HEAD, bytes_accessed=16 * rows * features
        ),
    )(tile_mask.reshape(7), query, key, value, grad_out)


def solution(mesh):
    spec = P(("grp", "seq"), None)
    return jax.shard_map(
        functools.partial(local, mesh.shape["seq"]),
        mesh=mesh,
        in_specs=(spec,) * 4 + (P("seq", None, None, None),),
        out_specs=(spec,) * 4,
        check_vma=False,
    )
```

```python
import functools

import jax
import jax.numpy as jnp
from jax import lax
from jax.experimental import pallas as pl
from jax.experimental.pallas import tpu as pltpu
from jax.sharding import PartitionSpec as P

HEAD = 128
HEADS_CHUNK = 5
BIG = 1e30
AHEAD = 1

OWN, SIB, CROSS, NEAR, DIAG, ZF, ZB = range(7)
C_SIB, C_CROSS, C_NEAR, C_DIAG_A, C_DIAG_B, C_ZF, C_ZB = range(7)
NT = (((1,), (1,)), ((), ()))


def kernel(seq, mask_ref, q_ref, k_ref, v_ref, g_ref, out_ref,
           rb, held, bias, stat_s, stat_r, load_sem, store_sem, send_sem, recv_sem, stat_send, stat_recv):
    rows = q_ref.shape[0]
    width = HEADS_CHUNK * HEAD
    chunks = q_ref.shape[1] // width
    steps = 2 * chunks
    scale = HEAD ** (-0.5)

    me = lax.axis_index("seq")
    core = lax.rem(me, 2)
    parity = lax.rem(lax.div(me, 2), 2)
    s = 1 - 2 * parity
    sib = me + 1 - 2 * core
    cross = me - 1 + 2 * core
    near, diag, zf, zb = me + 2 * s, me - 2 * s, me + 4 * s, me - 4 * s
    cross_ok = jnp.logical_and(cross >= 0, cross < seq)
    zf_ok = jnp.logical_and(zf >= 0, zf < seq)
    zb_ok = jnp.logical_and(zb >= 0, zb < seq)
    cross_send_ok = jnp.logical_or(core == parity, zb_ok)
    cross_src = jnp.where(core == parity, NEAR, DIAG)
    always = me >= 0
    target = {SIB: sib, CROSS: cross, NEAR: near, DIAG: diag, ZF: zf, ZB: zb}
    exists = {SIB: always, CROSS: cross_ok, NEAR: always, DIAG: zb_ok, ZF: zf_ok, ZB: zb_ok}
    reverse = {SIB: SIB, CROSS: CROSS, NEAR: NEAR, DIAG: DIAG, ZF: ZB, ZB: ZF}
    dist = {
        OWN: 0, SIB: 1 + core, CROSS: 2 - core, NEAR: 3 + parity, DIAG: 4 - parity,
        ZF: 5 + parity, ZB: 6 - parity,
    }

    def loads(t):
        first, second = ((k_ref, v_ref), (q_ref, g_ref))[t // chunks]
        cols = pl.ds(t % chunks * width, width)
        return [
            pltpu.make_async_copy(ref.at[:, cols], rb.at[OWN, t, j], load_sem.at[j, t])
            for j, ref in enumerate((first, second))
        ]

    for t in range(steps):
        for copy in loads(t):
            copy.start()

    barrier = pltpu.get_barrier_semaphore()
    for slot in (SIB, CROSS, NEAR, DIAG, ZF, ZB):
        @pl.when(exists[slot])
        def _(slot=slot):
            pl.semaphore_signal(barrier, inc=1, device_id={"seq": target[slot]})

    for slot in range(7):
        amount = (1.0 - mask_ref[dist[slot]].astype(jnp.float32)) * BIG
        bias[slot] = jnp.zeros((8, 128), jnp.float32) + amount

    peers = sum(jnp.where(exists[slot], 1, 0) for slot in (SIB, CROSS, NEAR, DIAG, ZF, ZB))
    pl.semaphore_wait(barrier, peers)

    def pair(slot, t):
        return rb.at[slot, t]

    def half(slot, which, t):
        return rb.at[slot, t, which]

    def copy_of(kind, t):
        if kind == C_SIB:
            src, dst, device = pair(OWN, t), pair(SIB, t), sib
        elif kind == C_NEAR:
            src, dst, device = pair(OWN, t), pair(NEAR, t), near
        elif kind == C_ZB:
            src, dst, device = pair(OWN, t), pair(ZB, t), zf
        elif kind == C_ZF:
            src, dst, device = pair(OWN, t), pair(ZF, t), zb
        elif kind == C_DIAG_A:
            src, dst, device = half(NEAR, 0, t), half(DIAG, 0, t), zf
        elif kind == C_DIAG_B:
            src, dst, device = half(ZF, 1, t), half(DIAG, 1, t), near
        else:
            src, dst, device = pair(cross_src, t), pair(CROSS, t), sib
        return pltpu.make_async_remote_copy(
            src_ref=src, dst_ref=dst, send_sem=send_sem.at[kind, t], recv_sem=recv_sem.at[kind, t],
            device_id={"seq": device}, device_id_type=pl.DeviceIdType.MESH,
        )

    sends = {
        C_SIB: always, C_CROSS: cross_send_ok, C_NEAR: always, C_DIAG_A: zf_ok, C_DIAG_B: zf_ok,
        C_ZF: zb_ok, C_ZB: zf_ok,
    }
    receives = {
        C_SIB: always, C_CROSS: cross_ok, C_NEAR: always, C_DIAG_A: zb_ok, C_DIAG_B: zb_ok,
        C_ZF: zf_ok, C_ZB: zb_ok,
    }

    def start(kind, t):
        @pl.when(sends[kind])
        def _():
            copy_of(kind, t).start()

    def arrived(kind, t):
        @pl.when(receives[kind])
        def _():
            copy_of(kind, t).wait_recv()

    def direct(t):
        for kind in (C_ZB, C_ZF, C_NEAR, C_SIB):
            start(kind, t)

    def stat_copy(slot, chunk):
        return pltpu.make_async_remote_copy(
            src_ref=stat_s.at[slot, chunk], dst_ref=stat_r.at[reverse[slot], chunk],
            send_sem=stat_send.at[slot, chunk], recv_sem=stat_recv.at[reverse[slot], chunk],
            device_id={"seq": target[slot]}, device_id_type=pl.DeviceIdType.MESH,
        )

    def stat_arrival(slot, chunk):
        return pltpu.make_async_remote_copy(
            src_ref=stat_s.at[slot, chunk], dst_ref=stat_r.at[slot, chunk],
            send_sem=stat_send.at[slot, chunk], recv_sem=stat_recv.at[slot, chunk],
            device_id={"seq": target[slot]}, device_id_type=pl.DeviceIdType.MESH,
        )

    def stacked(t, which, index):
        return rb[:, t, which, :, index * HEAD:(index + 1) * HEAD].reshape(7 * rows, HEAD)

    def own(t, which, index):
        return rb[OWN, t, which, :, index * HEAD:(index + 1) * HEAD]

    def result_copy(j, chunk):
        cols = pl.ds(pl.multiple_of(chunk * width, width), width)
        return pltpu.make_async_copy(held.at[j, chunk], out_ref.at[j, :, cols], store_sem.at[j, chunk])

    def query_side(chunk):
        lane = lax.broadcasted_iota(jnp.int32, (rows, 128), 1)
        stats = jnp.zeros((rows, 128), jnp.float32)
        shift = jnp.concatenate([bias[slot][:1, :] for slot in range(7)], axis=1)
        for index in range(HEADS_CHUNK):
            cols = slice(index * HEAD, (index + 1) * HEAD)
            keys, values = stacked(chunk, 0, index), stacked(chunk, 1, index)
            queries, grads = own(chunk + chunks, 0, index), own(chunk + chunks, 1, index)
            scores = lax.dot_general(queries, keys, NT, preferred_element_type=jnp.float32)
            scores = scores * scale - shift
            top = jnp.max(scores, axis=1, keepdims=True)
            weights = jnp.exp(scores - top)
            total = jnp.sum(weights, axis=1, keepdims=True)
            exact = weights * (1.0 / total)
            out = jnp.dot(exact.astype(jnp.bfloat16), values, preferred_element_type=jnp.float32)
            out = out.astype(jnp.bfloat16)
            held[0, chunk, :, cols] = out
            delta = jnp.sum(grads.astype(jnp.float32) * out.astype(jnp.float32), axis=1, keepdims=True)
            dprobs = lax.dot_general(grads, values, NT, preferred_element_type=jnp.float32)
            dscores = (exact * (dprobs - delta)).astype(jnp.bfloat16)
            grad = jnp.dot(dscores, keys, preferred_element_type=jnp.float32) * scale
            held[1, chunk, :, cols] = grad.astype(jnp.bfloat16)
            stats = jnp.where(lane == index, top + jnp.log(total), stats)
            stats = jnp.where(lane == index + 8, delta, stats)
        result_copy(0, chunk).start()
        result_copy(1, chunk).start()
        turned = jnp.transpose(stats)
        lse, delta = turned[:8], turned[8:16]
        stat_r[OWN, chunk] = jnp.concatenate([lse, delta], axis=0)
        for slot in (SIB, CROSS, NEAR, DIAG, ZF, ZB):
            stat_s[slot, chunk] = jnp.concatenate([lse + bias[slot], delta], axis=0)
        for slot in (SIB, CROSS, NEAR, DIAG, ZF, ZB):
            @pl.when(exists[slot])
            def _(slot=slot):
                stat_copy(slot, chunk).start()

    def key_side(chunk):
        for slot in (SIB, CROSS, NEAR, DIAG, ZF, ZB):
            @pl.when(exists[slot])
            def _(slot=slot):
                stat_arrival(slot, chunk).wait_recv()
        stats = jnp.concatenate([stat_r[slot, chunk] for slot in range(7)], axis=1)
        for index in range(HEADS_CHUNK):
            cols = slice(index * HEAD, (index + 1) * HEAD)
            queries, grads = stacked(chunk + chunks, 0, index), stacked(chunk + chunks, 1, index)
            keys, values = own(chunk, 0, index), own(chunk, 1, index)
            lse, delta = stats[index:index + 1], stats[index + 8:index + 9]
            scores = lax.dot_general(keys, queries, NT, preferred_element_type=jnp.float32)
            exact = jnp.exp(scores * scale - lse)
            value_grad = jnp.dot(exact.astype(jnp.bfloat16), grads, preferred_element_type=jnp.float32)
            held[3, chunk, :, cols] = value_grad.astype(jnp.bfloat16)
            dprobs = lax.dot_general(values, grads, NT, preferred_element_type=jnp.float32)
            dscores = (exact * (dprobs - delta)).astype(jnp.bfloat16)
            key_grad = jnp.dot(dscores, queries, preferred_element_type=jnp.float32) * scale
            held[2, chunk, :, cols] = key_grad.astype(jnp.bfloat16)
        result_copy(2, chunk).start()
        result_copy(3, chunk).start()

    for t in range(steps):
        for copy in loads(t):
            copy.wait()
        if t < AHEAD:
            direct(t)

    for slot in (CROSS, DIAG, ZF, ZB):
        @pl.when(jnp.logical_not(exists[slot]))
        def _(slot=slot):
            rb[slot] = jnp.zeros(rb.shape[1:], rb.dtype)
            stat_r[slot] = jnp.full(stat_r.shape[1:], BIG, jnp.float32)

    def step(t, carry):
        @pl.when(t + AHEAD < steps)
        def _():
            direct(t + AHEAD)

        @pl.when(t < steps)
        def _():
            arrived(C_NEAR, t)
            start(C_DIAG_A, t)
            arrived(C_ZF, t)
            start(C_DIAG_B, t)

        @pl.when(t >= 2)
        def _():
            arrived(C_SIB, t - 2)
            arrived(C_ZB, t - 2)
            arrived(C_CROSS, t - 2)

        @pl.when(jnp.logical_and(t >= 2, t - 2 < chunks))
        def _():
            query_side(t - 2)

        @pl.when(t - 2 >= chunks)
        def _():
            key_side(t - 2 - chunks)

        @pl.when(jnp.logical_and(t >= 1, t <= steps))
        def _():
            arrived(C_DIAG_A, t - 1)
            arrived(C_DIAG_B, t - 1)
            start(C_CROSS, t - 1)

        return carry

    lax.fori_loop(0, steps + 2, step, 0)

    def drain(t, carry):
        for kind in range(7):
            @pl.when(sends[kind])
            def _(kind=kind):
                copy_of(kind, t).wait_send()
        return carry

    lax.fori_loop(0, steps, drain, 0)

    def drain_stats(chunk, carry):
        for slot in (SIB, CROSS, NEAR, DIAG, ZF, ZB):
            @pl.when(exists[slot])
            def _(slot=slot):
                stat_copy(slot, chunk).wait_send()
        for j in range(4):
            result_copy(j, chunk).wait()
        return carry

    lax.fori_loop(0, chunks, drain_stats, 0)


def local(seq, query, key, value, grad_out, tile_mask):
    rows, features = query.shape
    chunks = features // (HEADS_CHUNK * HEAD)
    shape = jax.ShapeDtypeStruct((rows, features), jnp.bfloat16)
    anywhere = pl.BlockSpec(memory_space=pl.ANY)
    pairs = rows * rows * features * 7
    results = pl.pallas_call(
        functools.partial(kernel, seq),
        name="radial",
        out_shape=jax.ShapeDtypeStruct((4, rows, features), jnp.bfloat16),
        in_specs=[pl.BlockSpec(memory_space=pltpu.SMEM)] + [anywhere] * 4,
        out_specs=pl.BlockSpec(memory_space=pltpu.HBM),
        scratch_shapes=[
            pltpu.VMEM((7, 2 * chunks, 2, rows, HEADS_CHUNK * HEAD), jnp.bfloat16),
            pltpu.VMEM((4, chunks, rows, HEADS_CHUNK * HEAD), jnp.bfloat16),
            pltpu.VMEM((7, 8, 128), jnp.float32),
            pltpu.VMEM((7, chunks, 16, 128), jnp.float32),
            pltpu.VMEM((7, chunks, 16, 128), jnp.float32),
            pltpu.SemaphoreType.DMA((2, 2 * chunks)),
            pltpu.SemaphoreType.DMA((4, chunks)),
            pltpu.SemaphoreType.DMA((7, 2 * chunks)),
            pltpu.SemaphoreType.DMA((7, 2 * chunks)),
            pltpu.SemaphoreType.DMA((7, chunks)),
            pltpu.SemaphoreType.DMA((7, chunks)),
        ],
        compiler_params=pltpu.CompilerParams(
            collective_id=0, has_side_effects=True, vmem_limit_bytes=62 << 20
        ),
        cost_estimate=pl.CostEstimate(
            flops=16 * pairs, transcendentals=2 * pairs // HEAD, bytes_accessed=16 * rows * features
        ),
    )(tile_mask.reshape(7), query, key, value, grad_out)
    return tuple(results[j] for j in range(4))


def solution(mesh):
    spec = P(("grp", "seq"), None)
    return jax.shard_map(
        functools.partial(local, mesh.shape["seq"]),
        mesh=mesh,
        in_specs=(spec,) * 4 + (P("seq", None, None, None),),
        out_specs=(spec,) * 4,
        check_vma=False,
    )
```

```python
import functools

import jax
import jax.numpy as jnp
from jax import lax
from jax.experimental import pallas as pl
from jax.experimental.pallas import tpu as pltpu
from jax.sharding import PartitionSpec as P

HEAD = 128
HEADS_CHUNK = 5
BIG = 1e30
AHEAD = 1

OWN, SIB, CROSS, NEAR, DIAG, ZF, ZB = range(7)
C_SIB, C_CROSS, C_NEAR, C_DIAG_A, C_DIAG_B, C_ZF, C_ZB = range(7)
NT = (((1,), (1,)), ((), ()))


def kernel(seq, mask_ref, q_ref, k_ref, v_ref, g_ref, out_ref,
           rb, held, bias, stat_s, stat_r, load_sem, store_sem, send_sem, recv_sem, stat_send, stat_recv):
    rows = q_ref.shape[0]
    width = HEADS_CHUNK * HEAD
    chunks = q_ref.shape[1] // width
    steps = 2 * chunks
    scale = HEAD ** (-0.5)

    me = lax.axis_index("seq")
    core = lax.rem(me, 2)
    parity = lax.rem(lax.div(me, 2), 2)
    s = 1 - 2 * parity
    sib = me + 1 - 2 * core
    cross = me - 1 + 2 * core
    near, diag, zf, zb = me + 2 * s, me - 2 * s, me + 4 * s, me - 4 * s
    cross_ok = jnp.logical_and(cross >= 0, cross < seq)
    zf_ok = jnp.logical_and(zf >= 0, zf < seq)
    zb_ok = jnp.logical_and(zb >= 0, zb < seq)
    cross_send_ok = jnp.logical_or(core == parity, zb_ok)
    cross_src = jnp.where(core == parity, NEAR, DIAG)
    always = me >= 0
    target = {SIB: sib, CROSS: cross, NEAR: near, DIAG: diag, ZF: zf, ZB: zb}
    exists = {SIB: always, CROSS: cross_ok, NEAR: always, DIAG: zb_ok, ZF: zf_ok, ZB: zb_ok}
    reverse = {SIB: SIB, CROSS: CROSS, NEAR: NEAR, DIAG: DIAG, ZF: ZB, ZB: ZF}
    dist = {
        OWN: 0, SIB: 1 + core, CROSS: 2 - core, NEAR: 3 + parity, DIAG: 4 - parity,
        ZF: 5 + parity, ZB: 6 - parity,
    }

    def loads(t):
        first, second = ((k_ref, v_ref), (q_ref, g_ref))[t // chunks]
        cols = pl.ds(t % chunks * width, width)
        return [
            pltpu.make_async_copy(ref.at[:, cols], rb.at[OWN, t, j], load_sem.at[j, t])
            for j, ref in enumerate((first, second))
        ]

    for t in range(steps):
        for copy in loads(t):
            copy.start()

    barrier = pltpu.get_barrier_semaphore()
    for slot in (SIB, CROSS, NEAR, DIAG, ZF, ZB):
        @pl.when(exists[slot])
        def _(slot=slot):
            pl.semaphore_signal(barrier, inc=1, device_id={"seq": target[slot]})

    for slot in range(7):
        amount = (1.0 - mask_ref[dist[slot]].astype(jnp.float32)) * BIG
        bias[slot] = jnp.zeros((8, 128), jnp.float32) + amount

    peers = sum(jnp.where(exists[slot], 1, 0) for slot in (SIB, CROSS, NEAR, DIAG, ZF, ZB))
    pl.semaphore_wait(barrier, peers)

    def pair(slot, t):
        return rb.at[slot, t]

    def half(slot, which, t):
        return rb.at[slot, t, which]

    def copy_of(kind, t):
        if kind == C_SIB:
            src, dst, device = pair(OWN, t), pair(SIB, t), sib
        elif kind == C_NEAR:
            src, dst, device = pair(OWN, t), pair(NEAR, t), near
        elif kind == C_ZB:
            src, dst, device = pair(OWN, t), pair(ZB, t), zf
        elif kind == C_ZF:
            src, dst, device = pair(OWN, t), pair(ZF, t), zb
        elif kind == C_DIAG_A:
            src, dst, device = half(NEAR, 0, t), half(DIAG, 0, t), zf
        elif kind == C_DIAG_B:
            src, dst, device = half(ZF, 1, t), half(DIAG, 1, t), near
        else:
            src, dst, device = pair(cross_src, t), pair(CROSS, t), sib
        return pltpu.make_async_remote_copy(
            src_ref=src, dst_ref=dst, send_sem=send_sem.at[kind, t], recv_sem=recv_sem.at[kind, t],
            device_id={"seq": device}, device_id_type=pl.DeviceIdType.MESH,
        )

    sends = {
        C_SIB: always, C_CROSS: cross_send_ok, C_NEAR: always, C_DIAG_A: zf_ok, C_DIAG_B: zf_ok,
        C_ZF: zb_ok, C_ZB: zf_ok,
    }
    receives = {
        C_SIB: always, C_CROSS: cross_ok, C_NEAR: always, C_DIAG_A: zb_ok, C_DIAG_B: zb_ok,
        C_ZF: zf_ok, C_ZB: zb_ok,
    }

    def start(kind, t):
        @pl.when(sends[kind])
        def _():
            copy_of(kind, t).start()

    def arrived(kind, t):
        @pl.when(receives[kind])
        def _():
            copy_of(kind, t).wait_recv()

    def direct(t):
        for kind in (C_NEAR, C_ZF, C_ZB, C_SIB):
            start(kind, t)

    def stat_copy(slot, chunk):
        return pltpu.make_async_remote_copy(
            src_ref=stat_s.at[slot, chunk], dst_ref=stat_r.at[reverse[slot], chunk],
            send_sem=stat_send.at[slot, chunk], recv_sem=stat_recv.at[reverse[slot], chunk],
            device_id={"seq": target[slot]}, device_id_type=pl.DeviceIdType.MESH,
        )

    def stat_arrival(slot, chunk):
        return pltpu.make_async_remote_copy(
            src_ref=stat_s.at[slot, chunk], dst_ref=stat_r.at[slot, chunk],
            send_sem=stat_send.at[slot, chunk], recv_sem=stat_recv.at[slot, chunk],
            device_id={"seq": target[slot]}, device_id_type=pl.DeviceIdType.MESH,
        )

    def stacked(t, which, index):
        return rb[:, t, which, :, index * HEAD:(index + 1) * HEAD].reshape(7 * rows, HEAD)

    def own(t, which, index):
        return rb[OWN, t, which, :, index * HEAD:(index + 1) * HEAD]

    def result_copy(j, chunk):
        cols = pl.ds(pl.multiple_of(chunk * width, width), width)
        return pltpu.make_async_copy(held.at[j, chunk], out_ref.at[j, :, cols], store_sem.at[j, chunk])

    def query_side(chunk):
        lane = lax.broadcasted_iota(jnp.int32, (rows, 128), 1)
        stats = jnp.zeros((rows, 128), jnp.float32)
        shift = jnp.concatenate([bias[slot][:1, :] for slot in range(7)], axis=1)
        for index in range(HEADS_CHUNK):
            cols = slice(index * HEAD, (index + 1) * HEAD)
            keys, values = stacked(chunk, 0, index), stacked(chunk, 1, index)
            queries, grads = own(chunk + chunks, 0, index), own(chunk + chunks, 1, index)
            scores = lax.dot_general(queries, keys, NT, preferred_element_type=jnp.float32)
            scores = scores * scale - shift
            top = jnp.max(scores, axis=1, keepdims=True)
            weights = jnp.exp(scores - top)
            total = jnp.sum(weights, axis=1, keepdims=True)
            exact = weights * (1.0 / total)
            out = jnp.dot(exact.astype(jnp.bfloat16), values, preferred_element_type=jnp.float32)
            out = out.astype(jnp.bfloat16)
            held[0, chunk, :, cols] = out
            delta = jnp.sum(grads.astype(jnp.float32) * out.astype(jnp.float32), axis=1, keepdims=True)
            dprobs = lax.dot_general(grads, values, NT, preferred_element_type=jnp.float32)
            dscores = (exact * (dprobs - delta)).astype(jnp.bfloat16)
            grad = jnp.dot(dscores, keys, preferred_element_type=jnp.float32) * scale
            held[1, chunk, :, cols] = grad.astype(jnp.bfloat16)
            stats = jnp.where(lane == index, top + jnp.log(total), stats)
            stats = jnp.where(lane == index + 8, delta, stats)
        result_copy(0, chunk).start()
        result_copy(1, chunk).start()
        turned = jnp.transpose(stats)
        lse, delta = turned[:8], turned[8:16]
        stat_r[OWN, chunk] = jnp.concatenate([lse, delta], axis=0)
        for slot in (SIB, CROSS, NEAR, DIAG, ZF, ZB):
            stat_s[slot, chunk] = jnp.concatenate([lse + bias[slot], delta], axis=0)
        for slot in (SIB, CROSS, NEAR, DIAG, ZF, ZB):
            @pl.when(exists[slot])
            def _(slot=slot):
                stat_copy(slot, chunk).start()

    def key_side(chunk):
        for slot in (SIB, CROSS, NEAR, DIAG, ZF, ZB):
            @pl.when(exists[slot])
            def _(slot=slot):
                stat_arrival(slot, chunk).wait_recv()
        stats = jnp.concatenate([stat_r[slot, chunk] for slot in range(7)], axis=1)
        for index in range(HEADS_CHUNK):
            cols = slice(index * HEAD, (index + 1) * HEAD)
            queries, grads = stacked(chunk + chunks, 0, index), stacked(chunk + chunks, 1, index)
            keys, values = own(chunk, 0, index), own(chunk, 1, index)
            lse, delta = stats[index:index + 1], stats[index + 8:index + 9]
            scores = lax.dot_general(keys, queries, NT, preferred_element_type=jnp.float32)
            exact = jnp.exp(scores * scale - lse)
            value_grad = jnp.dot(exact.astype(jnp.bfloat16), grads, preferred_element_type=jnp.float32)
            held[3, chunk, :, cols] = value_grad.astype(jnp.bfloat16)
            dprobs = lax.dot_general(values, grads, NT, preferred_element_type=jnp.float32)
            dscores = (exact * (dprobs - delta)).astype(jnp.bfloat16)
            key_grad = jnp.dot(dscores, queries, preferred_element_type=jnp.float32) * scale
            held[2, chunk, :, cols] = key_grad.astype(jnp.bfloat16)
        result_copy(2, chunk).start()
        result_copy(3, chunk).start()

    for t in range(steps):
        for copy in loads(t):
            copy.wait()
        if t < AHEAD:
            direct(t)

    for slot in (CROSS, DIAG, ZF, ZB):
        @pl.when(jnp.logical_not(exists[slot]))
        def _(slot=slot):
            rb[slot] = jnp.zeros(rb.shape[1:], rb.dtype)
            stat_r[slot] = jnp.full(stat_r.shape[1:], BIG, jnp.float32)

    def step(t, carry):
        @pl.when(t + AHEAD < steps)
        def _():
            direct(t + AHEAD)

        @pl.when(t < steps)
        def _():
            arrived(C_NEAR, t)
            start(C_DIAG_A, t)
            arrived(C_ZF, t)
            start(C_DIAG_B, t)

            @pl.when(core == parity)
            def _():
                copy_of(C_CROSS, t).start()

        @pl.when(t >= 2)
        def _():
            arrived(C_SIB, t - 2)
            arrived(C_ZB, t - 2)
            arrived(C_CROSS, t - 2)

        @pl.when(jnp.logical_and(t >= 2, t - 2 < chunks))
        def _():
            query_side(t - 2)

        @pl.when(t - 2 >= chunks)
        def _():
            key_side(t - 2 - chunks)

        @pl.when(jnp.logical_and(t >= 1, t <= steps))
        def _():
            arrived(C_DIAG_A, t - 1)
            arrived(C_DIAG_B, t - 1)

            @pl.when(jnp.logical_and(core != parity, zb_ok))
            def _():
                copy_of(C_CROSS, t - 1).start()

        return carry

    lax.fori_loop(0, steps + 2, step, 0)

    def drain(t, carry):
        for kind in range(7):
            @pl.when(sends[kind])
            def _(kind=kind):
                copy_of(kind, t).wait_send()
        return carry

    lax.fori_loop(0, steps, drain, 0)

    def drain_stats(chunk, carry):
        for slot in (SIB, CROSS, NEAR, DIAG, ZF, ZB):
            @pl.when(exists[slot])
            def _(slot=slot):
                stat_copy(slot, chunk).wait_send()
        for j in range(4):
            result_copy(j, chunk).wait()
        return carry

    lax.fori_loop(0, chunks, drain_stats, 0)


def local(seq, query, key, value, grad_out, tile_mask):
    rows, features = query.shape
    chunks = features // (HEADS_CHUNK * HEAD)
    shape = jax.ShapeDtypeStruct((rows, features), jnp.bfloat16)
    anywhere = pl.BlockSpec(memory_space=pl.ANY)
    pairs = rows * rows * features * 7
    results = pl.pallas_call(
        functools.partial(kernel, seq),
        name="radial",
        out_shape=jax.ShapeDtypeStruct((4, rows, features), jnp.bfloat16),
        in_specs=[pl.BlockSpec(memory_space=pltpu.SMEM)] + [anywhere] * 4,
        out_specs=pl.BlockSpec(memory_space=pltpu.HBM),
        scratch_shapes=[
            pltpu.VMEM((7, 2 * chunks, 2, rows, HEADS_CHUNK * HEAD), jnp.bfloat16),
            pltpu.VMEM((4, chunks, rows, HEADS_CHUNK * HEAD), jnp.bfloat16),
            pltpu.VMEM((7, 8, 128), jnp.float32),
            pltpu.VMEM((7, chunks, 16, 128), jnp.float32),
            pltpu.VMEM((7, chunks, 16, 128), jnp.float32),
            pltpu.SemaphoreType.DMA((2, 2 * chunks)),
            pltpu.SemaphoreType.DMA((4, chunks)),
            pltpu.SemaphoreType.DMA((7, 2 * chunks)),
            pltpu.SemaphoreType.DMA((7, 2 * chunks)),
            pltpu.SemaphoreType.DMA((7, chunks)),
            pltpu.SemaphoreType.DMA((7, chunks)),
        ],
        compiler_params=pltpu.CompilerParams(
            collective_id=0, has_side_effects=True, vmem_limit_bytes=62 << 20
        ),
        cost_estimate=pl.CostEstimate(
            flops=16 * pairs, transcendentals=2 * pairs // HEAD, bytes_accessed=16 * rows * features
        ),
    )(tile_mask.reshape(7), query, key, value, grad_out)
    return tuple(results[j] for j in range(4))


def solution(mesh):
    spec = P(("grp", "seq"), None)
    return jax.shard_map(
        functools.partial(local, mesh.shape["seq"]),
        mesh=mesh,
        in_specs=(spec,) * 4 + (P("seq", None, None, None),),
        out_specs=(spec,) * 4,
        check_vma=False,
    )
```
